256 devices in a mesh: dp: 16 (over z, core), expert: 16 (over y, x).
Axes of the slice: x: 4, y: 4, z: 8, core: 2. Of those that a mesh axis runs over, the one named last changes fastest.
Arguments:
- tokens: bfloat16 [32768, 2048], P(('dp', 'expert')), may hold values from -6 to 6
- routes: int32 [32768, 8], P(('dp', 'expert')), may hold values from 0 to 63, all different within a row; in each aligned block of 128 rows (0 to 127, 128 to 255, ...) at most 20 rows name the same one
- gate_codes: int32 [32768, 8], P(('dp', 'expert')), may hold values from 1 to 255
- w_gate: bfloat16 [64, 2048, 384], P('expert', 'dp'), may hold values from -0.125 to 0.125
- w_up: bfloat16 [64, 2048, 384], P('expert', 'dp'), may hold values from -0.125 to 0.125
- w_down: bfloat16 [64, 384, 2048], P('expert', None, 'dp'), may hold values from -0.3125 to 0.3125
Outputs:
- mixed: bfloat16 [32768, 2048], P(('dp', 'expert'))
The draws below stay inside these ranges and needn't reach their ends.
Inputs may be any that keep to these rules, and one draw needn't show every extreme that they name: `routes`: each token names 8 different experts; the 128 tokens of one device name any one expert at most 20 times, a bound that some block reaches.
All inputs are finite; a program needn't handle non-finite values.
Results may differ from the reference program's by a relative error of at most 0.0058.
Values may be sent and summed in bfloat16 or wider, within the bound.
No kernel may reach another device: no remote copies, remote signals or barrier semaphores. Data moves between devices by JAX's collectives and lax.ppermute only.
A program may use at most 128 MiB of HBM per device.

```python
import math
import jax
import jax.numpy as jnp
import numpy as np
from jax import lax

D = 2048
FF = 384
TOPK = 8
TOK_DEV = 128
EXPERTS = 64
CAP = 20
TOKENS = 32768
N_DP = 16
N_EXPERT = 16


def place_ends(drawn, key, least, top_value):
    index_at = [jax.random.randint(jax.random.fold_in(key, axis), (), 0, length) for axis, length in enumerate(drawn.shape)]
    main_axis = drawn.shape.index(max(drawn.shape))
    neighbour = index_at[:main_axis] + [(index_at[main_axis] + 1) % drawn.shape[main_axis]] + index_at[main_axis + 1:]
    return drawn.at[tuple(index_at)].set(least).at[tuple(neighbour)].set(top_value)


def levels(stream_key, extent, split, least, high):
    def one(axis_at, parts):
        steps = jax.random.uniform(jax.random.fold_in(jax.random.fold_in(stream_key, 6), axis_at), (parts,), jnp.float32, least / len(split), high / len(split))
        return jnp.repeat(jnp.exp(steps), extent[axis_at] // parts).reshape((-1,) + (1,) * (len(extent) - axis_at - 1))

    level = one(*split[0])
    for cut in split[1:]:
        level = level * one(*cut)
    return level


def routed_block(key, own, number, rows, number_of, top, bound, skew):
    order = jax.random.permutation(key, number_of)
    crowded, common = shares(number_of, rows * top, bound, skew, True), shares(number_of, rows * top, bound, skew, False)
    places = jnp.arange(number_of)

    def named(lengths, turn):
        used = int((lengths > 0).sum())
        fixed = max(1, used // 4)
        moved = fixed + (places - fixed + turn * (used - fixed)) % max(1, number_of - fixed)
        return jnp.zeros((number_of,), jnp.int32).at[order[jnp.where(places < fixed, places, moved)]].set(jnp.asarray(lengths, jnp.int32))

    lengths = jnp.where(number % 4 == 0, named(crowded, number // 4), named(common, number - number // 4 - 1))
    mixed = jax.random.permutation(jax.random.fold_in(own, 3), number_of)
    donor, sink = mixed[0:number_of // 2 * 2:2], mixed[1:number_of // 2 * 2:2]
    room = jnp.minimum(lengths[donor] - 1, bound - lengths[sink]) // 2
    room = jnp.where((donor == order[0]) | (sink == order[0]) | (lengths[sink] == 0), 0, jnp.maximum(room, 0))
    moved = jax.random.randint(jax.random.fold_in(own, 4), (number_of // 2,), 0, 1 << 20) % (room + 1)
    lengths = lengths.at[donor].add(-moved).at[sink].add(moved)
    labels = jnp.searchsorted(jnp.cumsum(lengths), jnp.arange(rows * top), side="right").astype(jnp.int32)
    listing = labels.reshape(top, rows).T
    listing = listing[jax.random.permutation(jax.random.fold_in(own, 1), rows)]
    turn = jax.random.randint(jax.random.fold_in(own, 2), (rows, 1), 0, top)
    return jnp.take_along_axis(listing, (jnp.arange(top)[None, :] + turn) % top, axis=1)


def shares(amount, total, bound, skew, full):
    weights = [(1 << 20) // math.isqrt(rank ** skew) + 1 for rank in range(1, amount + 1)]
    largest = bound if full else min(bound, max(-(-total // amount), total * weights[0] // sum(weights)))
    least = 1 if total - largest >= amount - 1 else 0
    holding, surplus = [largest] + [least] * (amount - 1), total - largest - least * (amount - 1)
    while surplus > 0:
        candidates = [i for i in range(1, amount) if holding[i] < largest] or [i for i in range(1, amount) if holding[i] < bound]
        pool, budget = sum([weights[i] for i in candidates]), surplus
        for i in candidates:
            addition = min(bound - holding[i], max(1, budget * weights[i] // pool), surplus)
            holding[i] = holding[i] + addition
            surplus = surplus - addition
    return np.array(holding)


def noise(rng, shape, scale, bound, shards=(), kind=jnp.bfloat16):
    gain = levels(rng, shape, shards, -0.22, 0.18) if shards else 1.0
    values = jax.random.normal(rng, shape, jnp.float32) * scale * gain
    return jnp.minimum(jnp.maximum(values, -bound), bound).astype(kind)


def setup_inputs(seed: int = 0) -> dict:
    key_list = jax.random.split(jax.random.key(seed), 7)
    tokens = noise(key_list[0], (TOKENS, D), 1.0, 6.0, ((0, 256),))
    routes_keys = jax.random.split(jax.random.fold_in(key_list[1], 1), TOKENS // TOK_DEV)
    routes_turns = jax.random.permutation(jax.random.fold_in(key_list[1], 3), TOKENS // TOK_DEV)
    routes = jax.vmap(lambda own, number: routed_block(jax.random.fold_in(key_list[1], 2), own, number, TOK_DEV, EXPERTS, TOPK, CAP, 2))(routes_keys, routes_turns).reshape((TOKENS, TOPK))
    gate_codes = place_ends(jax.random.randint(key_list[2], (TOKENS, TOPK), 1, 256), jax.random.fold_in(key_list[2], 1), 1, 255).astype(jnp.int32)
    w_gate = noise(key_list[3], (EXPERTS, D, FF), D ** -0.5, 0.125, ((0, 16), (1, 16)))
    w_up = noise(key_list[4], (EXPERTS, D, FF), D ** -0.5, 0.125, ((0, 16), (1, 16)))
    w_down = noise(key_list[5], (EXPERTS, FF, D), FF ** -0.5, 0.3125, ((0, 16), (2, 16)))
    return {"tokens": tokens, "routes": routes, "gate_codes": gate_codes, "w_gate": w_gate, "w_up": w_up, "w_down": w_down}


def reference(tokens, routes, gate_codes, w_gate, w_up, w_down):
    flat_e = routes.reshape(-1).astype(jnp.int32)
    order = jnp.argsort(flat_e, stable=True).astype(jnp.int32)
    counts = jnp.bincount(flat_e, length=EXPERTS).astype(jnp.int32)
    starts = (jnp.cumsum(counts) - counts).astype(jnp.int32)
    most = CAP * N_DP * N_EXPERT
    padded_order = jnp.concatenate([order, jnp.zeros((most,), jnp.int32)])
    codes = gate_codes.astype(jnp.float32)
    flat_w = (codes / jnp.sum(codes, axis=1, keepdims=True)).reshape(-1)

    def one_expert(acc, e):
        index = lax.dynamic_slice_in_dim(padded_order, starts[e], most)
        live = jnp.arange(most, dtype=jnp.int32) < counts[e]
        tok_idx = (index // TOPK).astype(jnp.int32)
        rows = tokens[tok_idx]
        gate = jnp.dot(rows, w_gate[e], preferred_element_type=jnp.float32)
        upval = jnp.dot(rows, w_up[e], preferred_element_type=jnp.float32)
        hidden = (jax.nn.silu(gate) * upval).astype(jnp.bfloat16)
        result = jnp.dot(hidden, w_down[e], preferred_element_type=jnp.float32).astype(jnp.bfloat16)
        scale = jnp.where(live, flat_w[index], jnp.zeros((), flat_w.dtype))
        acc = acc.at[tok_idx].add(scale[:, None] * result.astype(acc.dtype))
        return acc, None

    start_acc = jnp.zeros((TOKENS, D), jnp.float32)
    acc, unused = lax.scan(one_expert, start_acc, jnp.arange(EXPERTS, dtype=jnp.int32))
    return acc.astype(jnp.bfloat16)
```

```python
import jax
import jax.numpy as jnp
from jax import lax
from jax.experimental import pallas as pl
from jax.experimental.pallas import tpu as pltpu
from jax.sharding import Mesh, PartitionSpec as P

BF = jnp.bfloat16
F32 = jnp.float32
I32 = jnp.int32
TOK, WIDTH, TOPK = 128, 2048, 8
EXPERTS, SLOTS, FF = 64, 20, 384
ROWS = EXPERTS * SLOTS
PER_CORE = ROWS // 2
Z = 8
BLK = 128
ANY = pl.BlockSpec(memory_space=pl.ANY)
SMEM = pl.BlockSpec(memory_space=pltpu.SMEM)
BIG = 60 << 20


def slots_of(routes_t):
    order = ((routes_t >> 1) & 1) * 32 + (routes_t >> 2) * 2 + (routes_t & 1)
    every = lax.broadcasted_iota(I32, (EXPERTS, TOK), 0)
    member = jnp.zeros((EXPERTS, TOK), F32)
    for k in range(TOPK):
        member = member + jnp.where(every == order[k : k + 1, :], 1.0, 0.0)
    earlier = lax.broadcasted_iota(I32, (TOK, TOK), 0) < lax.broadcasted_iota(I32, (TOK, TOK), 1)
    before = jnp.dot(member.astype(BF), jnp.where(earlier, 1.0, 0.0).astype(BF), preferred_element_type=F32)
    rows = []
    for k in range(TOPK):
        own = jnp.where(every == order[k : k + 1, :], before, 0.0)
        slot = jnp.sum(own, axis=0, keepdims=True).astype(I32)
        rows.append(order[k : k + 1, :] * SLOTS + slot)
    return rows


def dispatch_kernel(routes_ref, tok_ref, out_ref, row_ref):
    step = pl.program_id(0)

    @pl.when(step == 0)
    def _():
        for k, row in enumerate(slots_of(routes_ref[...])):
            row_ref[k : k + 1, :] = row

    height = out_ref.shape[0]
    here = lax.broadcasted_iota(I32, (height, TOK), 0) + step * height
    pick = jnp.zeros((height, TOK), F32)
    for k in range(TOPK):
        pick = jnp.where(here == row_ref[k : k + 1, :], 1.0, pick)
    out_ref[...] = jnp.dot(pick.astype(BF), tok_ref[...], preferred_element_type=F32).astype(BF)


def dispatch(routes_t, tokens):
    height = 256
    return pl.pallas_call(
        dispatch_kernel,
        grid=(ROWS // height,),
        in_specs=[pl.BlockSpec((TOPK, TOK), lambda i: (0, 0)), pl.BlockSpec((TOK, WIDTH), lambda i: (0, 0))],
        out_specs=pl.BlockSpec((height, WIDTH), lambda i: (i, 0)),
        out_shape=jax.ShapeDtypeStruct((ROWS, WIDTH), BF),
        scratch_shapes=[pltpu.VMEM((TOPK, TOK), I32)],
        compiler_params=pltpu.CompilerParams(vmem_limit_bytes=BIG),
        cost_estimate=pl.CostEstimate(flops=2 * ROWS * TOK * WIDTH, transcendentals=0, bytes_accessed=8 << 20),
        name="dispatch",
    )(routes_t, tokens)


def mixing_kernel(routes_ref, codes_ref, out_ref):
    rows = slots_of(routes_ref[...])
    codes = codes_ref[...].astype(F32)
    for piece in range(ROWS // BLK):
        here = lax.broadcasted_iota(I32, (BLK, TOK), 0) + piece * BLK
        weight = jnp.zeros((BLK, TOK), F32)
        for k in range(TOPK):
            weight = jnp.where(here == rows[k], codes[k : k + 1, :], weight)
        out_ref[:, piece * BLK : (piece + 1) * BLK] = weight.T.astype(BF)


def mixing(routes_t, codes_t):
    return pl.pallas_call(
        mixing_kernel,
        out_shape=jax.ShapeDtypeStruct((TOK, ROWS), BF),
        compiler_params=pltpu.CompilerParams(vmem_limit_bytes=BIG),
        name="mixing",
    )(routes_t, codes_t)


def pack_kernel(place_ref, wg_ref, wu_ref, wd_ref, *rest):
    keep0, keep1, send0, send1, dn_keep, dn_send, gu_buf, dn_buf, in_sem, out_sem = rest
    core = place_ref[1]
    loads, stores = [], []
    for half in range(2):
        first = 2 * core if half == 0 else 2 * (1 - core)
        dn = (dn_keep, dn_send)[half]
        for x in range(2):
            gu = ((keep0, keep1), (send0, send1))[half][x]
            n = 2 * half + x
            loads += [
                (wg_ref.at[first + x], gu_buf.at[2 * n]),
                (wu_ref.at[first + x], gu_buf.at[2 * n + 1]),
                (wd_ref.at[first + x], dn_buf.at[n]),
            ]
            stores += [(gu_buf.at[2 * n], gu.at[0]), (gu_buf.at[2 * n + 1], gu.at[1]), (dn_buf.at[n], dn.at[x])]
    loads = [pltpu.make_async_copy(src, dst, in_sem.at[n]) for n, (src, dst) in enumerate(loads)]
    stores = [pltpu.make_async_copy(src, dst, out_sem.at[n]) for n, (src, dst) in enumerate(stores)]
    for copy in loads:
        copy.start()
    for load, store in zip(loads, stores):
        load.wait()
        store.start()
    for copy in stores:
        copy.wait()


def pack(place, w_gate, w_up, w_down):
    gu = jax.ShapeDtypeStruct((2, BLK, FF), BF)
    dn = jax.ShapeDtypeStruct((2, FF, BLK), BF)
    return pl.pallas_call(
        pack_kernel,
        in_specs=[SMEM, ANY, ANY, ANY],
        out_specs=[ANY] * 6,
        out_shape=[gu] * 4 + [dn] * 2,
        scratch_shapes=[
            pltpu.VMEM((8, BLK, FF), BF),
            pltpu.VMEM((4, FF, BLK), BF),
            pltpu.SemaphoreType.DMA((12,)),
            pltpu.SemaphoreType.DMA((12,)),
        ],
        cost_estimate=pl.CostEstimate(flops=0, transcendentals=0, bytes_accessed=5 << 20),
        name="pack",
    )(place, w_gate, w_up, w_down)


def origin(place_ref, core, step, passed):
    z = place_ref[0]
    there = lax.rem(jnp.where(core == 0, z + Z - step, z + step), Z)
    return 2 * there + (core if passed == 0 else 1 - core)


CHUNK = 320


def hidden_kernel(place_ref, x_ref, *rest, expert):
    pieces, (out_ref, w_ref, sems) = rest[: 2 * Z], rest[2 * Z :]
    step = pl.program_id(0)

    @pl.when(step == 0)
    def _():
        core = place_ref[1]
        copies = []
        for n, piece in enumerate(pieces):
            at = pl.multiple_of(origin(place_ref, core, n // 2, n % 2) * BLK, BLK)
            for part in range(2):
                target = w_ref.at[pl.ds(at, BLK), pl.ds(part * FF, FF)]
                copies.append(pltpu.make_async_copy(piece.at[part], target, sems.at[2 * n + part]))
        for copy in copies:
            copy.start()
        for copy in copies:
            copy.wait()

    both = jnp.dot(x_ref[...], w_ref[...], preferred_element_type=F32)
    gate, up = both[:, :FF], both[:, FF:]
    value = gate / (1.0 + jnp.exp(-gate)) * up
    second = lax.rem(lax.broadcasted_iota(I32, (CHUNK, FF), 0), 2 * SLOTS) >= SLOTS
    mine = second if expert else jnp.logical_not(second)
    out_ref[...] = jnp.where(mine, value, 0.0).astype(BF)


def hidden_of(place, arrived, pieces, expert):
    def kernel(*refs):
        hidden_kernel(*refs, expert=expert)

    return pl.pallas_call(
        kernel,
        grid=(ROWS // CHUNK,),
        in_specs=[SMEM, pl.BlockSpec((CHUNK, WIDTH), lambda i: (i, 0))] + [ANY] * (2 * Z),
        out_specs=pl.BlockSpec((CHUNK, FF), lambda i: (i, 0)),
        out_shape=jax.ShapeDtypeStruct((ROWS, FF), BF),
        scratch_shapes=[pltpu.VMEM((WIDTH, 2 * FF), BF), pltpu.SemaphoreType.DMA((4 * Z,))],
        compiler_params=pltpu.CompilerParams(vmem_limit_bytes=BIG),
        cost_estimate=pl.CostEstimate(flops=4 * ROWS * WIDTH * FF, transcendentals=ROWS * FF, bytes_accessed=10 << 20),
        name="hidden",
    )(place, arrived, *pieces)


def down_kernel(h0_ref, h1_ref, *rest):
    pieces, (out_ref, w_ref, sems) = rest[:-3], rest[-3:]

    @pl.when(pl.program_id(0) == 0)
    def _():
        copies = []
        for n, piece in enumerate(pieces):
            for l in range(2):
                copies.append(
                    pltpu.make_async_copy(
                        piece.at[l], w_ref.at[pl.ds(l * FF, FF), pl.ds(n * BLK, BLK)], sems.at[2 * n + l]
                    )
                )
        for copy in copies:
            copy.start()
        for copy in copies:
            copy.wait()

    total = jnp.dot(h0_ref[...], w_ref[:FF, :], preferred_element_type=F32)
    total = total + jnp.dot(h1_ref[...], w_ref[FF:, :], preferred_element_type=F32)
    out_ref[...] = total.astype(BF)


def down(hidden, pieces):
    columns = len(pieces) * BLK
    return pl.pallas_call(
        down_kernel,
        grid=(ROWS // CHUNK,),
        in_specs=[pl.BlockSpec((CHUNK, FF), lambda i: (i, 0))] * 2 + [ANY] * len(pieces),
        out_specs=pl.BlockSpec((CHUNK, columns), lambda i: (i, 0)),
        out_shape=jax.ShapeDtypeStruct((ROWS, columns), BF),
        scratch_shapes=[pltpu.VMEM((2 * FF, columns), BF), pltpu.SemaphoreType.DMA((2 * len(pieces),))],
        compiler_params=pltpu.CompilerParams(vmem_limit_bytes=BIG),
        cost_estimate=pl.CostEstimate(flops=4 * ROWS * FF * columns, transcendentals=0, bytes_accessed=6 << 20),
        name="down",
    )(*hidden, *pieces)


def gather_part(place_ref, mix_ref, back_ref, total_ref, steps):
    for core in range(2):
        rows = slice(core * PER_CORE, (core + 1) * PER_CORE)
        part = jnp.dot(mix_ref[:, rows], back_ref[rows, :], preferred_element_type=F32)
        for n in range(2 * len(steps)):
            at = pl.multiple_of(origin(place_ref, core, steps[n // 2], n % 2) * BLK, BLK)
            total_ref[:, pl.ds(at, BLK)] = total_ref[:, pl.ds(at, BLK)] + part[:, n * BLK : (n + 1) * BLK]


def combine_first(place, mix, back, steps):
    def kernel(place_ref, mix_ref, back_ref, total_ref):
        total_ref[...] = jnp.zeros_like(total_ref)
        gather_part(place_ref, mix_ref, back_ref, total_ref, steps)

    return pl.pallas_call(
        kernel,
        in_specs=[SMEM, pl.BlockSpec(), pl.BlockSpec()],
        out_shape=jax.ShapeDtypeStruct((TOK, WIDTH), F32),
        compiler_params=pltpu.CompilerParams(vmem_limit_bytes=BIG),
        name="combine_first",
    )(place, mix, back)


def combine_last(place, mix, back, total, steps):
    def kernel(place_ref, mix_ref, back_ref, first_ref, out_ref, total_ref):
        total_ref[...] = first_ref[...]
        gather_part(place_ref, mix_ref, back_ref, total_ref, steps)
        code_sum = jnp.sum(mix_ref[...].astype(F32), axis=1, keepdims=True)
        out_ref[...] = (total_ref[...] / code_sum).astype(BF)

    return pl.pallas_call(
        kernel,
        in_specs=[SMEM] + [pl.BlockSpec()] * 3,
        out_shape=jax.ShapeDtypeStruct((TOK, WIDTH), BF),
        scratch_shapes=[pltpu.VMEM((TOK, WIDTH), F32)],
        compiler_params=pltpu.CompilerParams(vmem_limit_bytes=BIG),
        name="combine_last",
    )(place, mix, back, total)


RING = [(2 * z, 2 * ((z + 1) % Z)) for z in range(Z)] + [(2 * z + 1, 2 * ((z - 1) % Z) + 1) for z in range(Z)]
CROSS = [(2 * z + 1, 2 * ((z + 1) % Z)) for z in range(Z)] + [(2 * z, 2 * ((z - 1) % Z) + 1) for z in range(Z)]
SWAP = [(0, 1), (1, 0)]
SPLIT = 4


def ring(kept, sent):
    pieces = [kept, lax.ppermute(sent, "c", SWAP)]
    for step in range(Z - 1):
        kept = lax.ppermute(kept, ("z", "c"), RING)
        sent = lax.ppermute(sent, ("z", "c"), RING if step else CROSS)
        pieces += [kept, sent]
    return pieces


def exchange(rows):
    return lax.all_to_all(rows, ("c", "e"), split_axis=0, concat_axis=0, tiled=True)


def on_device(tokens, routes, gate_codes, w_gate, w_up, w_down):
    place = jnp.stack([lax.axis_index("z"), lax.axis_index("c")]).astype(I32)
    routes_t, codes_t = routes.T, gate_codes.T
    keep0, keep1, send0, send1, dn_keep, dn_send = pack(place, w_gate, w_up, w_down)
    tokens, keep0, keep1, send0, send1 = lax.optimization_barrier((tokens, keep0, keep1, send0, send1))
    gu = ring(keep0, send0), ring(keep1, send1)
    arrived = exchange(dispatch(routes_t, tokens))
    dn_keep, dn_send, gu[1][12] = lax.optimization_barrier((dn_keep, dn_send, gu[1][12]))
    dn = ring(dn_keep, dn_send)
    mix = mixing(routes_t, codes_t)
    hidden = [hidden_of(place, arrived, gu[x], x) for x in range(2)]
    back_first = exchange(down(hidden, dn[: 2 * SPLIT]))
    back_last = exchange(down(hidden, dn[2 * SPLIT :]))
    total = combine_first(place, mix, back_first, range(SPLIT))
    return combine_last(place, mix, back_last, total, range(SPLIT, Z))


def solution(mesh):
    fine = Mesh(mesh.devices.reshape(Z, 2, 16), ("z", "c", "e"))
    tok = P(("z", "c", "e"), None)
    return jax.shard_map(
        on_device,
        mesh=fine,
        in_specs=(tok, tok, tok, P("e", ("z", "c"), None), P("e", ("z", "c"), None), P("e", None, ("z", "c"))),
        out_specs=tok,
        check_vma=False,
    )
```
